32 devices in a mesh: pair: 16 (over z, x, core), virt: 2 (over y).
Axes of the slice: x: 2, y: 2, z: 4, core: 2. Of those that a mesh axis runs over, the one named last changes fastest.
Arguments:
- amplitudes: bfloat16 [80, 512, 512], P('pair', 'virt'), may hold values from -6 to 6
- cycle_inter: bfloat16 [48, 512, 512], P('pair', 'virt'), may hold values from -0.5 to 0.5
- pair_orbitals: int32 [80, 2], P('pair'), may hold values from 0 to 47, as said below
- occ_irrep: int32 [48], replicated, may hold values from 0 to 7
- virt_irrep: int32 [512], replicated, may hold values from 0 to 7
Outputs:
- residual: bfloat16 [80, 512, 512], P('pair', 'virt')
The draws below stay inside these ranges and needn't reach their ends.
Inputs may be any that keep to these rules, and one draw needn't show every extreme that they name: `pair_orbitals`: each row (i, j) has i < j, and no two rows are equal.
All inputs are finite; a program needn't handle non-finite values.
Results may differ from the reference program's by a relative error of at most 0.001.
Values may be sent and summed in bfloat16 or wider, within the bound.
No kernel may reach another device: no remote copies, remote signals or barrier semaphores. Data moves between devices by JAX's collectives and lax.ppermute only.
A program may use at most 64 MiB of HBM per device.

```python
import jax
import jax.numpy as jnp
from jax import lax

V = 512
ORBS = 48
PAIRS = 80


def draw_pair_orbitals(key, part):
    count = ORBS * ORBS
    order = jax.random.permutation(key, jnp.arange(count, dtype=jnp.int32))
    first = order // ORBS
    second = order % ORBS
    invalid = (first >= second).astype(jnp.int32)
    keep = jnp.argsort(invalid, stable=True)[:PAIRS]
    chosen = order[keep]
    return jnp.stack([chosen // ORBS, chosen % ORBS], axis=1).astype(jnp.int32)


def place_ends(drawn, key, low, high):
    extent = drawn.shape
    place = [jax.random.randint(jax.random.fold_in(key, axis), (), 0, extent[axis]) for axis in range(len(extent))]
    drawn = drawn.at[tuple(place)].set(low)
    longest = extent.index(max(extent))
    place[longest] = (place[longest] + 1) % extent[longest]
    return drawn.at[tuple(place)].set(high)


def block_levels(key, shape, pieces, smallest, top_value):
    factor_of, own = 1.0, jax.random.fold_in(key, 6)
    for axis_at, shards_of in pieces:
        draws = jnp.exp(jax.random.uniform(jax.random.fold_in(own, axis_at), (shards_of,), jnp.float32, smallest / len(pieces), top_value / len(pieces)))
        factor_of = factor_of * jnp.repeat(draws, shape[axis_at] // shards_of).reshape([-1 if axis == axis_at else 1 for axis in range(len(shape))])
    return factor_of


def bell_draw(key, shape, deviation, reach, pieces=(), held_as=jnp.bfloat16):
    loudness = block_levels(key, shape, pieces, -0.22, 0.18) if pieces else 1.0
    entries = jax.random.normal(key, shape, jnp.float32) * deviation * loudness
    return jnp.minimum(jnp.maximum(entries, -reach), reach).astype(held_as)


def setup_inputs(seed: int = 0) -> dict:
    key_list = jax.random.split(jax.random.key(seed), 6)
    return {
        "amplitudes": bell_draw(key_list[0], (PAIRS, V, V), 1.0, 6.0, ((0, 16), (1, 2))),
        "cycle_inter": bell_draw(key_list[1], (ORBS, V, V), (V // 4) ** -0.5, 0.5, ((0, 16), (1, 2))),
        "pair_orbitals": draw_pair_orbitals(jax.random.fold_in(key_list[5], 71), 0),
        "occ_irrep": place_ends(jax.random.randint(key_list[3], (ORBS,), 0, 8), jax.random.fold_in(key_list[3], 1), 0, 7).astype(jnp.int32),
        "virt_irrep": place_ends(jax.random.randint(key_list[4], (V,), 0, 8), jax.random.fold_in(key_list[4], 1), 0, 7).astype(jnp.int32),
    }


def reference(amplitudes, cycle_inter, pair_orbitals, occ_irrep, virt_irrep):
    block_diag = virt_irrep[:, None] == virt_irrep[None, :]
    block_sym = jnp.bitwise_xor(virt_irrep[:, None], virt_irrep[None, :])
    zero_bf = jnp.zeros((), jnp.bfloat16)

    def one_pair(items):
        orbitals, amp = items
        first = orbitals[0]
        second = orbitals[1]
        symmetry = jnp.bitwise_xor(occ_irrep[first], occ_irrep[second])
        masked_t = jnp.where(block_sym == symmetry, amp, zero_bf)
        g_second = jnp.where(block_diag, cycle_inter[second], zero_bf)
        g_first = jnp.where(block_diag, cycle_inter[first], zero_bf)
        total = jnp.dot(masked_t, g_second, preferred_element_type=jnp.float32)
        total = total + jnp.dot(g_first.T, masked_t, preferred_element_type=jnp.float32)
        return total.astype(jnp.bfloat16)

    return lax.map(one_pair, (pair_orbitals, amplitudes))
```

```python
import functools

import jax
import jax.numpy as jnp
import numpy as np
from jax import lax
from jax.experimental import pallas as pl
from jax.experimental.pallas import tpu as pltpu
from jax.sharding import PartitionSpec as P

IRREPS = 8
CAP = 96
F32 = jnp.float32
BF16 = jnp.bfloat16
ANY = pl.BlockSpec(memory_space=pl.ANY)
SMEM = pl.BlockSpec(memory_space=pltpu.SMEM)
VMEM = pl.BlockSpec(memory_space=pltpu.VMEM)


def dot(a, b, ca, cb):
    return lax.dot_general(a, b, (((ca,), (cb,)), ((), ())), preferred_element_type=F32)


def chip_ring(mesh):
    devices = list(mesh.devices[:, 0])
    count = len(devices)
    try:
        coords = [tuple(d.coords) for d in devices]
    except AttributeError:
        coords = [(i // 2,) for i in range(count)]
    chips = sorted(set(coords))
    varying = [a for a in range(len(chips[0])) if len({c[a] for c in chips}) > 1]
    order = None
    if len(varying) == 2:
        first = sorted({c[varying[0]] for c in chips})
        second = sorted({c[varying[1]] for c in chips})
        if len(first) % 2:
            first, second, varying = second, first, varying[::-1]
        if len(first) % 2 == 0 and len(first) * len(second) == len(chips):
            path = []
            for row, f in enumerate(first):
                inner = second[1:] if row % 2 == 0 else second[:0:-1]
                path += [(f, s) for s in inner]
            path += [(f, second[0]) for f in first[::-1]]
            order = {p: n for n, p in enumerate(path)}
    if order is None:
        position = {c: n for n, c in enumerate(chips)}
    else:
        position = {c: order[(c[varying[0]], c[varying[1]])] for c in chips}
    place, core, seen = [], [], {}
    for c in coords:
        place.append(position[c])
        core.append(seen.get(c, 0))
        seen[c] = core[-1] + 1
    return place, core


def one_hot_rows(irrep, symmetry=0):
    labels = lax.broadcasted_iota(jnp.int32, (IRREPS, irrep.shape[1]), 0)
    return (jnp.bitwise_xor(irrep, symmetry) == labels).astype(BF16)


def tables(irrep, start, slab, cap):
    size = irrep.shape[1]
    hot = one_hot_rows(irrep)
    below = lax.broadcasted_iota(jnp.int32, (size, size), 0) < lax.broadcasted_iota(
        jnp.int32, (size, size), 1
    )
    counted = dot(hot, below.astype(BF16), 1, 0)
    rank = jnp.sum(counted * hot.astype(F32), axis=0, keepdims=True).astype(jnp.int32)
    ranks = (lax.broadcasted_iota(jnp.int32, (cap, size), 0) == rank).astype(BF16)
    pick = (
        lax.broadcasted_iota(jnp.int32, (size, slab), 0)
        == lax.broadcasted_iota(jnp.int32, (size, slab), 1) + start
    ).astype(BF16)
    hot_own = dot(hot, pick, 1, 0).astype(BF16)
    ranks_own = dot(ranks, pick, 1, 0).astype(BF16)
    return hot, hot_own, ranks, ranks_own


def compact_inter_kernel(irrep_ref, inter_ref, out_ref, ranks_ref, ranks_own_ref, hot_own_ref):
    count, slab, size = inter_ref.shape
    cap = out_ref.shape[1]
    start = lax.axis_index("virt") * slab
    hot, hot_own, ranks, ranks_own = tables(irrep_ref[...], start, slab, cap)
    ranks_ref[...] = ranks
    ranks_own_ref[...] = ranks_own
    hot_own_ref[...] = hot_own
    mask = dot(hot_own, hot, 0, 0).astype(BF16)
    for k in range(count):
        out_ref[k] = dot(ranks, inter_ref[k] * mask, 1, 1).astype(BF16)


def pair_symmetry(orbitals_ref, occ_ref, p):
    return jnp.bitwise_xor(occ_ref[orbitals_ref[p, 0]], occ_ref[orbitals_ref[p, 1]])


def compact_amp_kernel(orbitals_ref, occ_ref, irrep_ref, hot_own_ref, ranks_ref, amp_ref, out_ref):
    symmetry = pair_symmetry(orbitals_ref, occ_ref, pl.program_id(0))
    mask = dot(hot_own_ref[...], one_hot_rows(irrep_ref[...], symmetry), 0, 0).astype(BF16)
    out_ref[0] = dot(ranks_ref[...], amp_ref[0] * mask, 1, 1).astype(BF16)


def residual_kernel(
    pieces,
    ring,
    owned,
    width,
    orbitals_ref,
    occ_ref,
    place_ref,
    core_ref,
    irrep_ref,
    hot_own_ref,
    ranks_ref,
    ranks_own_ref,
    amp_ref,
    *refs,
):
    flat = list(refs)
    inter_refs = [[flat.pop(0) for _ in range(n)] for n in pieces]
    amp_refs = [flat.pop(0) for _ in pieces]
    out_ref, inter, amps, inter_sem, amp_sem = flat
    p = pl.program_id(0)
    pairs = pl.num_programs(0)
    me = lax.axis_index("pair")
    virt = lax.axis_index("virt")
    parts = len(pieces)

    def lanes(piece):
        if parts == 1:
            return pl.ds(0, width)
        where = lax.rem(virt + piece, parts)
        return pl.ds(pl.multiple_of(where * width, width), width)

    def amp_copy(pair, piece):
        return pltpu.make_async_copy(
            amp_refs[piece].at[pair], amps.at[pair, :, lanes(piece)], amp_sem.at[pair, piece]
        )

    def inter_copy(source, row, slot, piece):
        return pltpu.make_async_copy(
            source.at[row], inter.at[slot, :, lanes(piece)], inter_sem.at[slot, piece]
        )

    @pl.when(p == 0)
    def _():
        @pl.loop(0, 2 * pairs)
        def _(slot):
            orbital = orbitals_ref[slot // 2, slot % 2]
            owner = orbital // owned
            row = orbital - owner * owned
            gap = lax.rem(place_ref[me] - place_ref[owner] + ring, ring)
            which = gap + ring * (core_ref[me] != core_ref[owner]).astype(jnp.int32)
            for piece, sources in enumerate(inter_refs):
                if len(sources) == 1:
                    inter_copy(sources[0], slot, slot, piece).start()
                    continue
                for n, source in enumerate(sources):

                    @pl.when(which == n)
                    def _(source=source, piece=piece):
                        inter_copy(source, row, slot, piece).start()

        @pl.loop(0, pairs)
        def _(pair):
            for piece in range(parts):
                amp_copy(pair, piece).start()

    hot = one_hot_rows(irrep_ref[...])
    symmetry = pair_symmetry(orbitals_ref, occ_ref, p)
    hot_own = hot_own_ref[...]
    mask = dot(hot_own, one_hot_rows(irrep_ref[...], symmetry), 0, 0)
    diagonal = dot(hot_own, hot, 0, 0)
    masked = amp_ref[0] * mask.astype(BF16)
    for piece in range(parts):
        amp_copy(p, piece).wait()
        for end in range(2):
            inter_copy(inter_refs[piece][0], 0, 2 * p + end, piece).wait()
    total = dot(masked, inter[2 * p + 1], 1, 1)
    mirror = (dot(ranks_own_ref[...], inter[2 * p], 0, 0) * diagonal).astype(BF16)
    total = total + dot(mirror, amps[p], 1, 1)
    spread = dot(total.astype(BF16), ranks_ref[...], 1, 0)
    out_ref[0] = (spread * mask).astype(BF16)


def blocked(cap, place, core, first_tables, amplitudes, inter_own, pair_orbitals, occ_irrep, irrep):
    ranks, ranks_own, hot_own = first_tables
    pairs, slab, size = amplitudes.shape
    owned = inter_own.shape[0]
    parts = lax.axis_size("virt")
    ring = len(place) // 2
    at = {(place[i], core[i]): i for i in range(len(place))}

    def hop(x, step):
        return lax.ppermute(
            x, "pair", [(i, at[(place[i] + step) % ring, core[i]]) for i in range(len(place))]
        )

    def swap(x):
        return lax.ppermute(x, "pair", [(i, at[place[i], 1 - core[i]]) for i in range(len(place))])

    def others(x):
        return [
            lax.ppermute(x, "virt", [((i + d) % parts, i) for i in range(parts)])
            for d in range(1, parts)
        ]

    def gathered(x, last):
        found = {0: x}
        ahead = behind = x
        for step in range(1, ring // 2):
            ahead, behind = hop(ahead, 1), hop(behind, -1)
            found[step], found[ring - step] = ahead, behind
        found[ring // 2] = hop(ahead if last > 0 else behind, last)
        mine = [found[d] for d in range(ring)]
        return mine + [swap(b) for b in mine]

    amps_own = pl.pallas_call(
        compact_amp_kernel,
        grid=(pairs,),
        in_specs=[SMEM, SMEM, VMEM, VMEM, VMEM, pl.BlockSpec((1, slab, size), lambda p: (p, 0, 0))],
        out_specs=pl.BlockSpec((1, cap, slab), lambda p: (p, 0, 0)),
        out_shape=jax.ShapeDtypeStruct((pairs, cap, slab), BF16),
        cost_estimate=pl.CostEstimate(
            flops=2 * pairs * cap * slab * size,
            bytes_accessed=2 * pairs * slab * (size + cap),
            transcendentals=0,
        ),
        name="compact_amp",
    )(pair_orbitals, occ_irrep, irrep, hot_own, ranks, amplitudes)

    amps_others = others(amps_own)
    width = slab
    if parts == 2 and slab % 128 == 0:
        inter_others = others(inter_own)
        inter_pieces = [gathered(inter_own, 1), gathered(inter_others[0], -1)]
        amp_pieces = [amps_own, amps_others[0]]
    else:
        width = slab * parts
        turn = jnp.remainder(jnp.arange(parts) - lax.axis_index("virt"), parts)

        def assembled(x, rest):
            whole = jnp.transpose(jnp.take(jnp.stack([x] + rest), turn, axis=0), (1, 2, 0, 3))
            return whole.reshape(x.shape[0], cap, width)

        every = lax.all_gather(inter_own, "pair", axis=0, tiled=True)
        chosen = jnp.take(every, pair_orbitals.reshape(-1), axis=0)
        inter_pieces = [[assembled(chosen, others(chosen))]]
        amp_pieces = [assembled(amps_own, amps_others)]

    operands = [b for piece in inter_pieces for b in piece] + amp_pieces
    kernel = functools.partial(
        residual_kernel, [len(piece) for piece in inter_pieces], ring, owned, width
    )
    row = pl.BlockSpec((1, slab, size), lambda p: (p, 0, 0))
    return pl.pallas_call(
        kernel,
        grid=(pairs,),
        in_specs=[SMEM] * 4 + [VMEM] * 4 + [row] + [ANY] * len(operands),
        out_specs=row,
        out_shape=jax.ShapeDtypeStruct((pairs, slab, size), BF16),
        scratch_shapes=[
            pltpu.VMEM((2 * pairs, cap, size), BF16),
            pltpu.VMEM((pairs, cap, size), BF16),
            pltpu.SemaphoreType.DMA((2 * pairs, len(inter_pieces))),
            pltpu.SemaphoreType.DMA((pairs, len(inter_pieces))),
        ],
        name="residual",
    )(
        pair_orbitals,
        occ_irrep,
        jnp.asarray(np.array(place, np.int32)),
        jnp.asarray(np.array(core, np.int32)),
        irrep,
        hot_own,
        ranks,
        ranks_own,
        amplitudes,
        *operands,
    )


def compact_inter(cap, cycle_inter, irrep):
    owned, slab, size = cycle_inter.shape
    return pl.pallas_call(
        compact_inter_kernel,
        in_specs=[VMEM, VMEM],
        out_specs=[VMEM] * 4,
        out_shape=[
            jax.ShapeDtypeStruct((owned, cap, slab), BF16),
            jax.ShapeDtypeStruct((cap, size), BF16),
            jax.ShapeDtypeStruct((cap, slab), BF16),
            jax.ShapeDtypeStruct((IRREPS, slab), BF16),
        ],
        name="compact_inter",
    )(irrep, cycle_inter)


def local(place, core, amplitudes, cycle_inter, pair_orbitals, occ_irrep, virt_irrep):
    size = amplitudes.shape[2]
    irrep = virt_irrep.reshape(1, size)
    labels = jnp.arange(IRREPS, dtype=jnp.int32)
    widest = jnp.max(jnp.sum((virt_irrep[None, :] == labels[:, None]).astype(jnp.int32), axis=1))

    def run(cap):
        inter_own, *first_tables = compact_inter(cap, cycle_inter, irrep)
        return blocked(
            cap, place, core, first_tables, amplitudes, inter_own, pair_orbitals, occ_irrep, irrep
        )

    cap = min(CAP, size)
    return lax.cond(widest <= cap, lambda: run(cap), lambda: run(size))


def solution(mesh):
    place, core = chip_ring(mesh)
    placed = (P("pair", "virt", None), P("pair", "virt", None), P("pair", None), P(), P())
    return jax.shard_map(
        functools.partial(local, place, core),
        mesh=mesh,
        in_specs=placed,
        out_specs=P("pair", "virt", None),
        check_vma=False,
    )
```
